32 devices in a mesh: groups: 2 (over y), prompt: 4 (over z), enc: 4 (over x, core).
Axes of the slice: x: 2, y: 2, z: 4, core: 2. Of those that a mesh axis runs over, the one named last changes fastest.
Arguments:
- embed: bfloat16 [8192, 256], P(('groups', 'prompt', 'enc')), parts along dimension 0, may hold values from -4000 to 4000
- coords: int32 [64, 6], P(('groups', 'prompt')), parts along dimension 0, may hold values from 0 to 1023
- targets: int32 [64], P(('groups', 'prompt')), parts along dimension 0, may hold values from 0 to 7
- counts: int32 [4], replicated, may hold values from 1 to 8, 16 in all
- labels: int32 [512, 256], P('groups'), parts along dimension 0, may hold values from 0 to 7
- type_embed: float32 [4, 256], replicated, may hold values from -5 to 5
- fourier: float32 [2, 128], replicated, may hold values from -5 to 5
- wq_t: bfloat16 [256, 128], replicated, may hold values from -0.375 to 0.375
- wk_t: bfloat16 [256, 128], replicated, may hold values from -0.375 to 0.375
- wv_t: bfloat16 [256, 128], replicated, may hold values from -0.375 to 0.375
- wo_t: bfloat16 [128, 256], replicated, may hold values from -0.5 to 0.5
- wq_i: bfloat16 [256, 128], replicated, may hold values from -0.375 to 0.375
- wk_i: bfloat16 [256, 128], replicated, may hold values from -0.375 to 0.375
- wv_i: bfloat16 [256, 128], replicated, may hold values from -0.375 to 0.375
- wo_i: bfloat16 [128, 256], replicated, may hold values from -0.5 to 0.5
- gain_one: float32 [256], replicated, may hold values from 0.1 to 1.9
- gain_two: float32 [256], replicated, may hold values from 0.1 to 1.9
- gain_three: float32 [64], replicated, may hold values from 0.1 to 1.9
- up_one: bfloat16 [256, 256], replicated, may hold values from -0.375 to 0.375
- second_upsample_weight: bfloat16 [64, 128], replicated, may hold values from -0.75 to 0.75
- hyper_one: bfloat16 [256, 256], replicated, may hold values from -0.375 to 0.375
- hyper_two: bfloat16 [256, 32], replicated, may hold values from -0.375 to 0.375
Outputs:
- grad_embed: float32 [8192, 256], P(('groups', 'prompt', 'enc')), parts along dimension 0
The draws below stay inside these ranges and needn't reach their ends.
There are 2 independent parts, one for each index of `groups`. The reference program is written for one: setup_inputs(seed, part) draws one part's arguments, and reference() takes and returns one part's arrays. A program takes and returns all parts, laid end to end along the dimension named above; an argument that names none is the same for every part. Nothing has to cross between parts.
Inputs may be any that keep to these rules, and one draw needn't show every extreme that they name: Prompt index p has counts[p] live prompts, in its first slots; the counts sum to 16 and the largest is 8.
All inputs are finite; a program needn't handle non-finite values.
Results may differ from the reference program's by a relative error of at most 0.0035.
Values may be sent and summed in bfloat16 or wider, within the bound.
No kernel may reach another device: no remote copies, remote signals or barrier semaphores. Data moves between devices by JAX's collectives and lax.ppermute only.
A program may use at most 128 MiB of HBM per device.

```python
import math
import jax
import jax.numpy as jnp
import numpy as np
from jax import lax

C = 256
ATT = 128
HEADS = 8
HD = 16
UPA = 64
UPB = 32
IMG = 1024
TOKENS = 4096
MASKSIDE = 256
SLOTS = 8
PROMPTS = 16
PSLOTS = 32
NOBJ = 8
TB = 256
N_PROMPT = 4
N_ENC = 4


def draw_embed(key, part):
    base_key, scale_key, column_key = jax.random.split(key, 3)
    rows = jnp.arange(TOKENS, dtype=jnp.int32)
    enc_place = (rows // TB % N_ENC).astype(jnp.float32)
    rise = (enc_place / (N_ENC - 1)).reshape(TOKENS, 1)
    base = jnp.clip(jax.random.normal(base_key, (TOKENS, C), jnp.float32), -5.0, 5.0)
    row_scale = jnp.exp(jax.random.uniform(scale_key, (TOKENS, 1), jnp.float32, -0.4, 0.4))
    row_scale = row_scale * jnp.exp(rise * math.log(3.0))
    column_scale = jnp.exp(jax.random.uniform(column_key, (1, C), jnp.float32, -0.3, 0.3))
    values = base * row_scale * column_scale
    return values.astype(jnp.bfloat16)


def plant(entries, key, low, high):
    longest = entries.shape.index(max(entries.shape))
    spots = []
    for shift in (0, 1):
        where = [jax.random.randint(jax.random.fold_in(key, axis), (), 0, length) for axis, length in enumerate(entries.shape)]
        where[longest] = (where[longest] + shift) % entries.shape[longest]
        spots.append(tuple(where))
    return entries.at[spots[0]].set(low).at[spots[1]].set(high)


def profile(count, total, bound, skew):
    loads = [(1 << 20) // math.isqrt(rank ** skew) + 1 for rank in range(2, count + 1)]
    spare, given = total - bound - (count - 1), [1] * (count - 1)
    while spare > 0:
        free = [i for i in range(count - 1) if given[i] < bound]
        mass, left = sum([loads[i] for i in free]), spare
        for i in free:
            more = min(bound - given[i], max(1, left * loads[i] // mass), spare)
            given[i] = given[i] + more
            spare = spare - more
    return np.array([bound] + given)


def ragged(key, amount, total, most, skew):
    if amount == 2:
        one = jax.random.randint(key, (), max(1, total - most), min(most, total - 1) + 1)
        return jnp.stack([one, total - one])
    lengths = jnp.asarray(profile(amount, total, most, skew), jnp.int32)
    couples = (amount - 1) // 2
    donor, taker = lengths[1:1 + 2 * couples:2], lengths[2:2 + 2 * couples:2]
    margin = jnp.minimum(donor - 1, most - taker)
    moved = jax.random.randint(jax.random.fold_in(key, 1), (couples,), 0, 1 << 20) % (margin + 1)
    lengths = lengths.at[1:1 + 2 * couples:2].set(donor - moved).at[2:2 + 2 * couples:2].set(taker + moved)
    return lengths[jax.random.permutation(jax.random.fold_in(key, 2), amount)]


def bell_draw(key, extent, scale, limit, kind=jnp.bfloat16):
    return jnp.clip(scale * jax.random.normal(key, extent, jnp.float32), -limit, limit).astype(kind)


def setup_inputs(seed: int = 0, part: int = 0) -> dict:
    splits = jax.random.split(jax.random.key(seed), 23)
    part_keys = jax.random.split(jax.random.fold_in(splits[22], part), 23)
    embed = draw_embed(jax.random.fold_in(jax.random.fold_in(splits[22], part), 71), part)
    coords = plant(jax.random.randint(part_keys[1], (PSLOTS, 6), 0, IMG), jax.random.fold_in(part_keys[1], 1), 0, IMG - 1).astype(jnp.int32)
    targets = plant(jax.random.randint(part_keys[2], (PSLOTS,), 0, NOBJ), jax.random.fold_in(part_keys[2], 1), 0, NOBJ - 1).astype(jnp.int32)
    counts = ragged(splits[3], N_PROMPT, PROMPTS, SLOTS, 2).astype(jnp.int32)
    labels = plant(jax.random.randint(part_keys[4], (MASKSIDE, MASKSIDE), 0, NOBJ), jax.random.fold_in(part_keys[4], 1), 0, NOBJ - 1).astype(jnp.int32)
    type_embed = bell_draw(splits[5], (4, C), 1.0, 5.0, jnp.float32)
    fourier = bell_draw(splits[6], (2, C // 2), 1.0, 5.0, jnp.float32)
    wq_t = bell_draw(splits[7], (C, ATT), C ** -0.5, 0.375)
    wk_t = bell_draw(splits[8], (C, ATT), C ** -0.5, 0.375)
    wv_t = bell_draw(splits[9], (C, ATT), C ** -0.5, 0.375)
    wo_t = bell_draw(splits[10], (ATT, C), ATT ** -0.5, 0.5)
    wq_i = bell_draw(splits[11], (C, ATT), C ** -0.5, 0.375)
    wk_i = bell_draw(splits[12], (C, ATT), C ** -0.5, 0.375)
    wv_i = bell_draw(splits[13], (C, ATT), C ** -0.5, 0.375)
    wo_i = bell_draw(splits[14], (ATT, C), ATT ** -0.5, 0.5)
    gain_one = jnp.clip(1.0 + 0.18 * jax.random.normal(splits[15], (C,), jnp.float32), 0.1, 1.9)
    gain_two = jnp.clip(1.0 + 0.18 * jax.random.normal(splits[16], (C,), jnp.float32), 0.1, 1.9)
    gain_three = jnp.clip(1.0 + 0.18 * jax.random.normal(splits[17], (UPA,), jnp.float32), 0.1, 1.9)
    up_one = bell_draw(splits[18], (C, 4 * UPA), C ** -0.5, 0.375)
    second_upsample_weight = bell_draw(splits[19], (UPA, 4 * UPB), UPA ** -0.5, 0.75)
    hyper_one = bell_draw(splits[20], (C, C), C ** -0.5, 0.375)
    hyper_two = bell_draw(splits[21], (C, UPB), C ** -0.5, 0.375)
    return {"embed": embed, "coords": coords, "targets": targets, "counts": counts, "labels": labels, "type_embed": type_embed, "fourier": fourier, "wq_t": wq_t, "wk_t": wk_t, "wv_t": wv_t, "wo_t": wo_t, "wq_i": wq_i, "wk_i": wk_i, "wv_i": wv_i, "wo_i": wo_i, "gain_one": gain_one, "gain_two": gain_two, "gain_three": gain_three, "up_one": up_one, "second_upsample_weight": second_upsample_weight, "hyper_one": hyper_one, "hyper_two": hyper_two}


highest_value = lax.Precision.HIGHEST
epsilon = 1e-05

def layer_norm(values, gain):
    centered = values - lax.optimization_barrier(jnp.mean(values, axis=-1, keepdims=True))
    variance = lax.optimization_barrier(jnp.mean(centered * centered, axis=-1, keepdims=True))
    return centered * lax.rsqrt(variance + epsilon) * gain

def fourier_code(pixel_pair, fourier):
    scaled = 2.0 * ((pixel_pair.astype(jnp.float32) + 0.5) / IMG) - 1.0
    angles = 2.0 * math.pi * jnp.dot(scaled, fourier, precision=highest_value)
    return jnp.concatenate([jnp.sin(angles), jnp.cos(angles)], axis=-1)

def prompt_tokens(corner_rows, type_embed, fourier):
    point_code = fourier_code(corner_rows[..., 0:2], fourier) + type_embed[1]
    first_code = fourier_code(corner_rows[..., 2:4], fourier) + type_embed[2]
    second_code = fourier_code(corner_rows[..., 4:6], fourier) + type_embed[3]
    output_token = jnp.broadcast_to(type_embed[0], point_code.shape)
    return jnp.stack([output_token, point_code, first_code, second_code], axis=-2)

def token_pixel_scores(labels):
    side = labels.shape[0] // 4
    grid_view = labels.reshape(side, 2, 2, side, 2, 2)
    grid_view = jnp.transpose(grid_view, (0, 3, 1, 4, 2, 5))
    return grid_view.reshape(side * side, 4, 4)

def token_side(tokens_zero, key_image, value_image, wq_t, wo_t, gain_one):
    head_scale = HD ** (-0.5)
    queries = jnp.dot(tokens_zero, wq_t.astype(jnp.float32), precision=highest_value).reshape(-1, HEADS, HD)
    scores = jnp.einsum('rhd,jhd->rhj', queries, key_image.reshape(-1, HEADS, HD), precision=highest_value) * head_scale
    attention = jax.nn.softmax(scores, axis=-1)
    gathered = jnp.einsum('rhj,jhd->rhd', attention, value_image.reshape(-1, HEADS, HD), precision=highest_value)
    update = jnp.dot(gathered.reshape(tokens_zero.shape[0], -1), wo_t.astype(jnp.float32), precision=highest_value)
    return layer_norm(tokens_zero + update, gain_one)

def image_side(query_image, image_float, tokens_one, truth, live_flag, side_weights):
    wk_i, wv_i, wo_i, gain_two, up_one, gain_three, second_upsample_weight, hyper_one, hyper_two = side_weights
    head_scale = HD ** (-0.5)
    row_count = query_image.shape[0]
    token_keys = jnp.dot(tokens_one, wk_i.astype(jnp.float32), precision=highest_value).reshape(-1, HEADS, HD)
    token_values = jnp.dot(tokens_one, wv_i.astype(jnp.float32), precision=highest_value).reshape(-1, HEADS, HD)
    scores = jnp.einsum('jhd,rhd->jhr', query_image.reshape(row_count, HEADS, HD), token_keys, precision=highest_value) * head_scale
    attention = jax.nn.softmax(scores, axis=-1)
    mixed = jnp.einsum('jhr,rhd->jhd', attention, token_values, precision=highest_value).reshape(row_count, -1).astype(jnp.bfloat16)
    update = jnp.dot(mixed, wo_i, preferred_element_type=jnp.float32)
    image_one = layer_norm(image_float + update, gain_two).astype(jnp.bfloat16)
    lifted = jnp.dot(image_one, up_one, preferred_element_type=jnp.float32).reshape(row_count, 4, -1)
    first_activation = jax.nn.gelu(layer_norm(lifted, gain_three), approximate=False).astype(jnp.bfloat16)
    second_result = jnp.einsum('oij,jp->oip', first_activation.astype(jnp.float32), second_upsample_weight.astype(jnp.float32), precision=highest_value)
    features = jax.nn.gelu(second_result, approximate=False).reshape(row_count, 4, 4, -1)
    hidden = jax.nn.relu(jnp.dot(tokens_one[0], hyper_one.astype(jnp.float32), precision=highest_value))
    hyper = jnp.dot(hidden, hyper_two.astype(jnp.float32), precision=highest_value)
    logits = jnp.einsum('tasc,c->tas', features, hyper, precision=highest_value)
    losses = jax.nn.softplus(logits) - truth * logits
    return jnp.sum(losses) * live_flag * 0.25

def reference(embed, coords, targets, counts, labels, type_embed, fourier, wq_t, wk_t, wv_t, wo_t, wq_i, wk_i, wv_i, wo_i, gain_one, gain_two, gain_three, up_one, second_upsample_weight, hyper_one, hyper_two):
    key_image = jnp.dot(embed, wk_t, preferred_element_type=jnp.float32)
    value_image = jnp.dot(embed, wv_t, preferred_element_type=jnp.float32)
    query_image = jnp.dot(embed, wq_i, preferred_element_type=jnp.float32)
    image_float = embed.astype(jnp.float32)
    pixels = token_pixel_scores(labels)
    ends = jnp.cumsum(counts).astype(jnp.int32)
    numbers = jnp.arange(PROMPTS, dtype=jnp.int32)
    owners = lax.optimization_barrier(jnp.sum((ends[None, :] <= numbers[:, None]).astype(jnp.int32), axis=1)).astype(jnp.int32)
    starts = jnp.take(ends, owners) - jnp.take(counts, owners)
    slot_index = (owners * SLOTS + numbers - starts).astype(jnp.int32)
    chosen_rows = jnp.take(coords, slot_index, axis=0)
    chosen_targets = jnp.take(targets, slot_index)
    side_weights = (wk_i, wv_i, wo_i, gain_two, up_one, gain_three, second_upsample_weight, hyper_one, hyper_two)

    def single_prompt(carry, inputs):
        corner_row, target = inputs
        tokens_zero = prompt_tokens(corner_row, type_embed, fourier)
        truth = (pixels == target).astype(jnp.float32)

        def loss_of(query_arg, key_arg, value_arg, image_arg):
            tokens_one = token_side(tokens_zero, key_arg, value_arg, wq_t, wo_t, gain_one)
            return image_side(query_arg, image_arg, tokens_one, truth, 1.0, side_weights)
        _, pullback = jax.vjp(loss_of, query_image, key_image, value_image, image_float)
        grads = pullback(jnp.ones((), jnp.float32))
        return (tuple((total + piece_grad for total, piece_grad in zip(carry, grads))), None)
    initial = (jnp.zeros_like(query_image), jnp.zeros_like(key_image), jnp.zeros_like(value_image), jnp.zeros_like(image_float))
    sums, _ = lax.scan(single_prompt, initial, (chosen_rows, chosen_targets))
    d_query, d_key, d_value, d_image = sums
    grad_embed = d_image + jnp.dot(d_query, wq_i.astype(jnp.float32).T, precision=highest_value)
    grad_embed = grad_embed + jnp.dot(d_key, wk_t.astype(jnp.float32).T, precision=highest_value)
    grad_embed = grad_embed + jnp.dot(d_value, wv_t.astype(jnp.float32).T, precision=highest_value)
    return grad_embed
```

```python
import functools
import math

import jax
import jax.numpy as jnp
from jax import lax
from jax.experimental import pallas as pl
from jax.experimental.pallas import tpu as pltpu
from jax.sharding import PartitionSpec as P

HEADS = 8
HD = 16
IMG = 1024
CHUNK = 16
TOK = 4 * CHUNK
COLS = 256
SCALE = HD ** (-0.5)
EPS = 1e-05
HIGH = lax.Precision.HIGHEST
F32 = jnp.float32
BF16 = jnp.bfloat16
VMEM_LIMIT = 56 * 1024 * 1024

NN = (((1,), (0,)), ((), ()))
NT = (((1,), (1,)), ((), ()))
TN = (((0,), (0,)), ((), ()))


def exact(a, b, dims=NN):
    return lax.dot_general(
        a.astype(F32), b.astype(F32), dims, precision=HIGH, preferred_element_type=F32
    )


def single(a, b, dims=NN):
    return lax.dot_general(a, b, dims, preferred_element_type=F32)


def parts(values):
    high = values.astype(BF16)
    rest = values - high.astype(F32)
    middle = rest.astype(BF16)
    low = (rest - middle.astype(F32)).astype(BF16)
    return high, middle, low


def head_mask(rows, head):
    lane = lax.broadcasted_iota(jnp.int32, (rows, 128), 1)
    return (lane // HD == head).astype(F32)


def by_head(values):
    return jnp.concatenate(
        [values * head_mask(values.shape[0], h) for h in range(HEADS)], axis=0
    )


def token_by_head(values):
    lane = lax.broadcasted_iota(jnp.int32, (1, HEADS, 128), 2)
    head = lax.broadcasted_iota(jnp.int32, (1, HEADS, 128), 1)
    mask = (lane // HD == head).astype(F32)
    return (values[:, None, :] * mask).reshape(values.shape[0] * HEADS, 128)


def fold_heads(values):
    count = values.shape[0] // HEADS
    lane = lax.broadcasted_iota(jnp.int32, (1, HEADS, 128), 2)
    head = lax.broadcasted_iota(jnp.int32, (1, HEADS, 128), 1)
    mask = (lane // HD == head).astype(F32)
    return jnp.sum(values.reshape(count, HEADS, 128) * mask, axis=1)


def prep_kernel(up, wo, w2, wv, g2, g3, up_t, wo_t, w2_t, wv_t, up3, wo3, w23, g2b, g3b):
    def turned(ref):
        return jnp.transpose(ref[...].astype(F32)).astype(BF16)

    up_t[...] = turned(up)
    wo_t[...] = turned(wo)
    w2_t[...] = turned(w2)
    wv_t[...] = turned(wv)
    for src, dst in ((up, up3), (wo, wo3), (w2, w23)):
        width = src.shape[1]
        for k in range(3):
            dst[:, k * width : (k + 1) * width] = src[...]
    for src, dst in ((g2, g2b), (g3, g3b)):
        column = jnp.transpose(jnp.broadcast_to(src[...], (128, src.shape[1])))
        for k in range(COLS // 128):
            dst[:, k * 128 : (k + 1) * 128] = column


def gather_kernel(
    nblocks,
    embed_rows,
    coded,
    rank,
    own,
    *refs,
):
    blocks = refs[:nblocks]
    (table, type_embed, fourier, wq, wk, wv, wv_t, wqi) = refs[nblocks : nblocks + 8]
    (payload, tokens, queries, live, key_own, value_own, query_t, embed_t) = refs[
        nblocks + 8 : nblocks + 16
    ]
    key_all, value_t = refs[nblocks + 16 :]
    chunk = pl.program_id(0)

    def first():
        for k in range(nblocks):
            rows = blocks[k][0:embed_rows, :]
            key_all[k * embed_rows : (k + 1) * embed_rows, :] = single(rows, wk[...])
            value_t[:, k * embed_rows : (k + 1) * embed_rows] = single(wv_t[...], rows, NT)
        mine = own[...]
        key_own[...] = single(mine, wk[...])
        value_own[...] = single(mine, wv[...])
        query_t[...] = jnp.transpose(single(mine, wqi[...]))
        embed_t[...] = jnp.transpose(mine.astype(F32))

    pl.when(chunk == 0)(first)

    if coded:
        pieces = []
        for k in range(nblocks):
            code = blocks[k][embed_rows : embed_rows + 16, 0:128].astype(F32)
            pieces.append(code[0:8] * 32.0 + code[8:16])
        slots = jnp.concatenate(pieces, axis=0)
    else:
        slots = table[...]
    slot_count = slots.shape[0]
    number = lax.broadcasted_iota(jnp.int32, (CHUNK, slot_count), 0) + chunk * CHUNK
    chosen = (number == rank[0:1, :]).astype(F32)
    rows = exact(chosen, slots)
    live[...] = rows
    scaled = 2.0 * ((rows + 0.5) / IMG) - 1.0
    two_pi = 2.0 * math.pi
    kinds = [jnp.broadcast_to(type_embed[0:1, :], (CHUNK, 256))]
    for r in range(3):
        across = scaled[:, 2 * r : 2 * r + 1] * fourier[0:1, :]
        down = scaled[:, 2 * r + 1 : 2 * r + 2] * fourier[1:2, :]
        angles = two_pi * (across + down)
        code = jnp.concatenate([jnp.sin(angles), jnp.cos(angles)], axis=-1)
        kinds.append(code + type_embed[r + 1 : r + 2, :])
    token_rows = jnp.concatenate(kinds, axis=0)
    tokens[...] = token_rows
    query_rows = exact(token_rows, wq[...])
    queries[...] = query_rows

    scores = exact(key_all[...], by_head(query_rows * SCALE), NT)
    top = jnp.max(scores, axis=0, keepdims=True)
    shifted = jnp.exp(scores - top)
    total = jnp.sum(shifted, axis=0, keepdims=True)
    gathered = exact(value_t[...], shifted)
    first_half = lax.broadcasted_iota(jnp.int32, (HD, 128), 1) < TOK
    for k in range(4):
        lanes = slice(128 * k, 128 * k + 128)
        even = gathered[32 * k : 32 * k + 16, lanes]
        odd = gathered[32 * k + 16 : 32 * k + 32, lanes]
        payload[0, HD * k : HD * k + HD, :] = jnp.where(first_half, even, odd)
        payload[0, 64 + k : 65 + k, :] = top[:, lanes]
        payload[0, 68 + k : 69 + k, :] = total[:, lanes]


def gelu_pair(x):
    phi = 0.5 + 0.5 * lax.erf(x * (0.5**0.5))
    bell = jnp.exp2(x * x * (-0.5 * math.log2(math.e)))
    return x * phi, phi + x * (bell * (1.0 / math.sqrt(2.0 * math.pi)))


def column_norm(values, count):
    centered = values - jnp.sum(values, axis=0, keepdims=True) * (1.0 / count)
    variance = jnp.sum(centered * centered, axis=0, keepdims=True) * (1.0 / count)
    inverse = lax.rsqrt(variance + EPS)
    return centered * inverse, inverse


def column_norm_pull(cotangent, normed, inverse, count):
    mean = jnp.sum(cotangent, axis=0, keepdims=True) * (1.0 / count)
    along = jnp.sum(cotangent * normed, axis=0, keepdims=True) * (1.0 / count)
    return inverse * (cotangent - mean - normed * along)


def prompt_kernel(
    senders,
    row_count,
    payload,
    tokens,
    live,
    embed_t,
    query_t,
    labels,
    wo_t,
    gain_one,
    wk_i,
    wv_i,
    wq_i,
    hyper_one,
    hyper_two,
    up_t,
    wo_i_t,
    w2_t,
    up3,
    wo3,
    w23,
    g2b,
    g3b,
    image_out,
    gathered_out,
    stat_out,
    pull_out,
    image_sum,
    score_ref,
    key_ref,
    value_ref,
    value_cat,
    score_grad,
    value_grad,
    hyper_ref,
    hyper_sum,
    target_ref,
):
    share = COLS // row_count
    blocks = CHUNK // share
    chunk = pl.program_id(0)
    lane = lax.broadcasted_iota(jnp.int32, (1, COLS), 1)

    def segment(p):
        return lane // row_count == p

    gathered_pieces = []
    half = TOK
    tops, totals = [], []
    for k in range(4):
        top = payload[0, 0, 64 + k : 65 + k, :]
        for d in range(1, senders):
            top = jnp.maximum(top, payload[d, 0, 64 + k : 65 + k, :])
        total = jnp.zeros_like(top)
        summed = jnp.zeros((HD, 128), F32)
        for d in range(senders):
            factor = jnp.exp(payload[d, 0, 64 + k : 65 + k, :] - top)
            total = total + payload[d, 0, 68 + k : 69 + k, :] * factor
            summed = summed + payload[d, 0, HD * k : HD * k + HD, :] * factor
        packed = summed / total
        gathered_pieces.append(packed[:, 0:half])
        gathered_pieces.append(packed[:, half : 2 * half])
        stat_out[0, k : k + 1, :] = top
        stat_out[0, 4 + k : 5 + k, :] = total
    gathered = jnp.transpose(jnp.concatenate(gathered_pieces, axis=0))
    gathered_out[...] = gathered

    summed = tokens[...] + exact(gathered, wo_t[...])
    centered = summed - jnp.mean(summed, axis=-1, keepdims=True)
    variance = jnp.mean(centered * centered, axis=-1, keepdims=True)
    token_inverse = lax.rsqrt(variance + EPS)
    token_normed = centered * token_inverse
    tokens_one = token_normed * gain_one[...]
    key_ref[...] = token_by_head(exact(tokens_one, wk_i[...]) * SCALE)
    value_rows = token_by_head(exact(tokens_one, wv_i[...]))
    value_ref[...] = value_rows.reshape(4, CHUNK, HEADS, 128)
    score_ref[...] = exact(key_ref[...], query_t[...]).reshape(4, CHUNK, HEADS, COLS)
    value_turned = jnp.transpose(
        jnp.transpose(value_rows.reshape(4, CHUNK, HEADS, 128), (1, 0, 2, 3)).reshape(
            CHUNK * 32, 128
        )
    )
    high, middle, low = parts(value_turned)
    for g in range(CHUNK):
        at = slice(32 * g, 32 * g + 32)
        value_cat[g] = jnp.concatenate(
            [high[:, at], high[:, at], high[:, at], middle[:, at], middle[:, at], low[:, at]],
            axis=1,
        )
    output_rows = jnp.broadcast_to(tokens_one[0:1, :], (128, 256))
    hidden = jnp.maximum(exact(output_rows, hyper_one[...]), 0.0)
    hyper_columns = jnp.transpose(exact(hidden, hyper_two[...]))
    for k in range(COLS // 128):
        hyper_ref[:, 128 * k : 128 * k + 128] = hyper_columns
    for b in range(blocks):
        row = jnp.broadcast_to(live[b * share : b * share + 1, 6:7], (1, COLS))
        for p in range(1, share):
            row = jnp.where(segment(p), live[b * share + p : b * share + p + 1, 6:7], row)
        target_ref[b] = row

    hyper_sum[...] = jnp.zeros_like(hyper_sum)

    def clear():
        image_sum[...] = jnp.zeros_like(image_sum)
        image_out[...] = jnp.zeros_like(image_out)

    pl.when(chunk == 0)(clear)

    def block(b, carry):
        base = b * share
        if share == 1:
            scores = score_ref[:, base]
        else:
            scores = score_ref[:, 0]
            for p in range(1, share):
                scores = jnp.where(segment(p), score_ref[:, p], scores)
        top = jnp.max(scores, axis=0, keepdims=True)
        raised = jnp.exp(scores - top)
        probs = raised / jnp.sum(raised, axis=0, keepdims=True)
        prob_rows = probs.reshape(32, COLS)
        ph, pm, pw = parts(prob_rows)
        stacked = jnp.concatenate([ph, pm, pw, ph, pm, ph], axis=0)
        mixed = single(value_cat[base], stacked)
        for p in range(1, share):
            mixed = jnp.where(segment(p), single(value_cat[p], stacked), mixed)
        mixed = mixed.astype(BF16)
        normed, inverse = column_norm(embed_t[...] + single(wo_i_t[...], mixed), 256)
        image_one = (normed * g2b[...]).astype(BF16)
        lifted = single(up_t[...], image_one)
        target = target_ref[b]
        lift_parts = []
        for a in range(4):
            normed3, inverse3 = column_norm(lifted[64 * a : 64 * a + 64], 64)
            act, act_slope = gelu_pair(normed3 * g3b[...])
            second = single(w2_t[...], act.astype(BF16))
            second_parts = []
            for pos in range(4):
                feature, slope = gelu_pair(second[32 * pos : 32 * pos + 32])
                logit = jnp.sum(feature * hyper_ref[...], axis=0, keepdims=True)
                truth = (labels[4 * a + pos : 4 * a + pos + 1, :] == target).astype(F32)
                d_logit = (lax.logistic(logit) - truth) * 0.25
                hyper_sum[...] += feature * d_logit
                second_parts.append(parts(hyper_ref[...] * slope * d_logit))
            stacked_second = jnp.concatenate(
                [second_parts[pos][k] for k in range(3) for pos in range(4)], axis=0
            )
            d_act = single(w23[...], stacked_second).astype(BF16).astype(F32)
            d_normed = d_act * act_slope * g3b[...]
            lift_parts.append(parts(column_norm_pull(d_normed, normed3, inverse3, 64)))
        stacked_lift = jnp.concatenate(
            [lift_parts[a][k] for k in range(3) for a in range(4)], axis=0
        )
        d_image_one = single(up3[...], stacked_lift).astype(BF16).astype(F32)
        d_sum = column_norm_pull(d_image_one * g2b[...], normed, inverse, 256)
        image_sum[...] += d_sum
        d_mixed = single(wo3[...], jnp.concatenate(parts(d_sum), axis=0)).astype(BF16)

        def for_prompt(g, prob_terms):
            value_terms = jnp.concatenate(parts(value_ref[:, g].reshape(32, 128)), axis=0)
            d_prob = single(value_terms, d_mixed)
            d_prob = d_prob[0:32] + d_prob[32:64] + d_prob[64:96]
            d_value = single(jnp.concatenate(prob_terms, axis=0), d_mixed, NT)
            d_value = d_value[0:32] + d_value[32:64] + d_value[64:96]
            value_grad[:, g] = d_value.reshape(4, HEADS, 128)
            return d_prob

        if share == 1:
            d_prob = for_prompt(base, (ph, pm, pw))
        else:
            d_prob = jnp.zeros((32, COLS), F32)
            for p in range(share):
                kept = jnp.where(segment(p), prob_rows, 0.0)
                d_prob = jnp.where(segment(p), for_prompt(p, parts(kept)), d_prob)
        d_prob = d_prob.reshape(4, HEADS, COLS)
        d_scores = probs * (d_prob - jnp.sum(probs * d_prob, axis=0, keepdims=True))
        if share == 1:
            score_grad[:, base] = d_scores
        else:
            for p in range(share):
                score_grad[:, p] = jnp.where(segment(p), d_scores, 0.0)
        return carry

    lax.fori_loop(0, blocks, block, 0)

    score_rows = score_grad[...].reshape(TOK * HEADS, COLS)
    d_query = exact(key_ref[...], score_rows, TN)
    image_out[...] += exact(wq_i[...], d_query)
    d_key = fold_heads(exact(score_rows, query_t[...], NT)) * SCALE
    d_value = fold_heads(value_grad[...].reshape(TOK * HEADS, 128))
    d_tokens = exact(d_key, wk_i[...], NT) + exact(d_value, wv_i[...], NT)
    d_hyper = exact(jnp.ones((8, COLS), F32), hyper_sum[...], NT)
    d_hidden = jnp.where(hidden[0:8] > 0.0, exact(d_hyper, hyper_two[...], NT), 0.0)
    d_output = exact(d_hidden, hyper_one[...], NT)
    row = lax.broadcasted_iota(jnp.int32, (TOK, 256), 0)
    d_tokens = d_tokens + jnp.where(row == 0, d_output[0:1, :], 0.0)
    d_normed = d_tokens * gain_one[...]
    mean = jnp.mean(d_normed, axis=-1, keepdims=True)
    along = jnp.mean(d_normed * token_normed, axis=-1, keepdims=True)
    d_summed = token_inverse * (d_normed - mean - token_normed * along)
    pull_out[...] = exact(d_summed, wo_t[...], NT)

    def finish():
        image_out[...] += image_sum[...]

    pl.when(chunk == pl.num_programs(0) - 1)(finish)


def final_kernel(
    count,
    key_own,
    value_own,
    queries,
    gathered,
    stats,
    image_grad,
    wk,
    wv,
    *refs,
):
    pulls = refs[:count]
    out = refs[count]
    key_grad, value_grad = refs[count + 1 :]
    chunk = pl.program_id(0)

    def clear():
        key_grad[...] = jnp.zeros_like(key_grad)
        value_grad[...] = jnp.zeros_like(value_grad)

    pl.when(chunk == 0)(clear)
    pull = pulls[0][...]
    for other in pulls[1:]:
        pull = pull + other[...]
    query_rows = by_head(queries[...] * SCALE)
    pull_rows = by_head(pull)
    delta = exact(jnp.ones((8, 128), F32), by_head(pull * gathered[...]), NT)[0:1, :]
    scores = exact(key_own[...], query_rows, NT)
    top = jnp.concatenate([stats[0, k : k + 1, :] for k in range(4)], axis=1)
    total = jnp.concatenate([stats[0, 4 + k : 5 + k, :] for k in range(4)], axis=1)
    probs = jnp.exp(scores - top) * (1.0 / total)
    d_probs = exact(value_own[...], pull_rows, NT)
    d_scores = probs * (d_probs - delta)
    key_grad[...] += exact(d_scores, query_rows)
    value_grad[...] += exact(probs, pull_rows)

    def finish():
        out[...] = (
            jnp.transpose(image_grad[...])
            + exact(key_grad[...], wk[...], NT)
            + exact(value_grad[...], wv[...], NT)
        )

    pl.when(chunk == pl.num_programs(0) - 1)(finish)


def whole(shape):
    return pl.BlockSpec(shape, lambda i: (0,) * len(shape))


def chunked(shape, axis=0):
    def index(i):
        return tuple(i if d == axis else 0 for d in range(len(shape)))

    return pl.BlockSpec(shape, index)


def params():
    return pltpu.CompilerParams(
        dimension_semantics=("arbitrary",), vmem_limit_bytes=VMEM_LIMIT
    )


def shape_of(shape, dtype=F32):
    return jax.ShapeDtypeStruct(shape, dtype)


def own_labels(labels, first_token, rows):
    side = labels.shape[1] // 4
    high = max(1, rows // side)
    wide = min(side, rows)
    top = first_token // side
    left = first_token % side
    piece = lax.dynamic_slice(labels, (4 * top, 4 * left), (4 * high, 4 * wide))
    piece = piece.reshape(high, 2, 2, wide, 2, 2)
    return jnp.transpose(piece, (1, 4, 2, 5, 0, 3)).reshape(16, rows)


def on_device(
    embed,
    coords,
    targets,
    counts,
    labels,
    type_embed,
    fourier,
    wq_t,
    wk_t,
    wv_t,
    wo_t,
    wq_i,
    wk_i,
    wv_i,
    wo_i,
    gain_one,
    gain_two,
    gain_three,
    up_one,
    second_upsample_weight,
    hyper_one,
    hyper_two,
):
    n_prompt = lax.axis_size("prompt")
    n_enc = lax.axis_size("enc")
    p = lax.axis_index("prompt")
    e = lax.axis_index("enc")
    rows = embed.shape[0]
    slots = coords.shape[0]
    chunks = n_prompt * slots // 2 // CHUNK
    share = COLS // rows
    direct = n_prompt == 4 and slots == 8 and rows >= 128

    table = jnp.concatenate([coords, targets[:, None]], axis=1)
    if direct:
        code = jnp.concatenate([table // 32, table % 32], axis=0).astype(BF16)
        code = jnp.pad(code, ((0, 0), (0, 256 - 7)))
        block = jnp.concatenate([embed, code], axis=0)
        blocks = [block]
        for k in range(1, 4):
            blocks.append(lax.ppermute(block, "prompt", [(i, i ^ k) for i in range(4)]))
        owners = jnp.bitwise_xor(p, jnp.arange(4, dtype=jnp.int32))
        block_rows = rows
        table_all = jnp.zeros((8, 128), F32)
    else:
        blocks = [lax.all_gather(embed, "prompt", axis=0, tiled=True)]
        table_all = lax.all_gather(table, "prompt", axis=0, tiled=True).astype(F32)
        table_all = jnp.pad(table_all, ((0, 0), (0, 128 - 7)))
        owners = jnp.arange(n_prompt, dtype=jnp.int32)
        block_rows = rows * n_prompt
    index = jnp.arange(n_prompt, dtype=jnp.int32)
    starts = jnp.sum(jnp.where(index[None, :] < owners[:, None], counts[None, :], 0), axis=1)
    sizes = jnp.sum(jnp.where(index[None, :] == owners[:, None], counts[None, :], 0), axis=1)
    slot = jnp.arange(slots, dtype=jnp.int32)[None, :]
    rank = jnp.where(slot < sizes[:, None], starts[:, None] + slot, -1)
    rank = jnp.broadcast_to(rank.reshape(1, n_prompt * slots), (8, n_prompt * slots))
    own = own_labels(labels, (p * n_enc + e) * rows, rows).astype(F32)
    if share > 1:
        own = jnp.tile(own, (1, share))

    prepared = pl.pallas_call(
        prep_kernel,
        out_shape=(
            shape_of((256, 256), BF16),
            shape_of((256, 128), BF16),
            shape_of((128, 64), BF16),
            shape_of((128, 256), BF16),
            shape_of((256, 768), BF16),
            shape_of((128, 768), BF16),
            shape_of((64, 384), BF16),
            shape_of((256, COLS)),
            shape_of((64, COLS)),
        ),
        name="prep",
    )(
        up_one,
        wo_i,
        second_upsample_weight,
        wv_t,
        gain_two.reshape(1, 256),
        gain_three.reshape(1, 64),
    )
    up_t, wo_i_t, w2_t, wv_turned, up3, wo3, w23, g2b, g3b = prepared

    all_rows = block_rows * len(blocks)
    gather_args = (
        rank,
        embed,
        *blocks,
        table_all,
        type_embed,
        fourier,
        wq_t,
        wk_t,
        wv_t,
        wv_turned,
        wq_i,
    )
    payload, tokens, queries, live, key_own, value_own, query_t, embed_t = pl.pallas_call(
        functools.partial(gather_kernel, len(blocks), block_rows, direct),
        grid=(chunks,),
        in_specs=[whole(a.shape) for a in gather_args],
        out_specs=(
            chunked((1, 72, 128)),
            chunked((TOK, 256)),
            chunked((TOK, 128)),
            chunked((CHUNK, 128)),
            whole((rows, 128)),
            whole((rows, 128)),
            whole((128, rows)),
            whole((256, rows)),
        ),
        out_shape=(
            shape_of((chunks, 72, 128)),
            shape_of((chunks * TOK, 256)),
            shape_of((chunks * TOK, 128)),
            shape_of((chunks * CHUNK, 128)),
            shape_of((rows, 128)),
            shape_of((rows, 128)),
            shape_of((128, rows)),
            shape_of((256, rows)),
        ),
        scratch_shapes=[pltpu.VMEM((all_rows, 128), F32), pltpu.VMEM((128, all_rows), F32)],
        compiler_params=params(),
        name="gather",
    )(*gather_args)

    payloads = lax.all_gather(payload, "enc")
    if share > 1:
        embed_t = jnp.tile(embed_t, (1, share))
        query_t = jnp.tile(query_t, (1, share))
    prompt_args = (
        payloads,
        tokens,
        live,
        embed_t,
        query_t,
        own,
        wo_t,
        gain_one.reshape(1, 256),
        wk_i,
        wv_i,
        wq_i,
        hyper_one,
        hyper_two,
        up_t,
        wo_i_t,
        w2_t,
        up3,
        wo3,
        w23,
        g2b,
        g3b,
    )
    prompt_specs = [whole(a.shape) for a in prompt_args]
    prompt_specs[0] = chunked((n_enc, 1, 72, 128), 1)
    prompt_specs[1] = chunked((TOK, 256))
    prompt_specs[2] = chunked((CHUNK, 128))
    image_grad, gathered, stats, pull = pl.pallas_call(
        functools.partial(prompt_kernel, n_enc, rows),
        grid=(chunks,),
        in_specs=prompt_specs,
        out_specs=(
            whole((256, COLS)),
            chunked((TOK, 128)),
            chunked((1, 8, 128)),
            chunked((TOK, 128)),
        ),
        out_shape=(
            shape_of((256, COLS)),
            shape_of((chunks * TOK, 128)),
            shape_of((chunks, 8, 128)),
            shape_of((chunks * TOK, 128)),
        ),
        scratch_shapes=[
            pltpu.VMEM((256, COLS), F32),
            pltpu.VMEM((4, CHUNK, HEADS, COLS), F32),
            pltpu.VMEM((TOK * HEADS, 128), F32),
            pltpu.VMEM((4, CHUNK, HEADS, 128), F32),
            pltpu.VMEM((CHUNK, 128, 192), BF16),
            pltpu.VMEM((4, CHUNK, HEADS, COLS), F32),
            pltpu.VMEM((4, CHUNK, HEADS, 128), F32),
            pltpu.VMEM((32, COLS), F32),
            pltpu.VMEM((32, COLS), F32),
            pltpu.VMEM((CHUNK // share, 1, COLS), F32),
        ],
        compiler_params=params(),
        name="prompts",
    )(*prompt_args)
    if share > 1:
        image_grad = jnp.sum(image_grad.reshape(256, share, rows), axis=1)

    pull = jnp.sum(lax.all_gather(pull, "enc"), axis=0)
    if n_prompt == 4:
        pulls = [pull]
        for k in range(1, 4):
            pulls.append(lax.ppermute(pull, "prompt", [(i, i ^ k) for i in range(4)]))
    else:
        pulls = [lax.psum(pull, "prompt")]

    final_args = (
        key_own,
        value_own,
        queries,
        gathered,
        stats,
        image_grad,
        wk_t,
        wv_t,
        *pulls,
    )
    final_specs = [whole(a.shape) for a in final_args]
    final_specs[2] = chunked((TOK, 128))
    final_specs[3] = chunked((TOK, 128))
    final_specs[4] = chunked((1, 8, 128))
    for k in range(len(pulls)):
        final_specs[8 + k] = chunked((TOK, 128))
    return pl.pallas_call(
        functools.partial(final_kernel, len(pulls)),
        grid=(chunks,),
        in_specs=final_specs,
        out_specs=whole((rows, 256)),
        out_shape=shape_of((rows, 256)),
        scratch_shapes=[pltpu.VMEM((rows, 128), F32), pltpu.VMEM((rows, 128), F32)],
        compiler_params=params(),
        name="final",
    )(*final_args)


def solution(mesh):
    in_specs = (
        P(("groups", "prompt", "enc"), None),
        P(("groups", "prompt"), None),
        P(("groups", "prompt")),
        P(),
        P("groups", None),
        *([P()] * 17),
    )
    out_specs = P(("groups", "prompt", "enc"), None)
    return jax.shard_map(
        on_device, mesh=mesh, in_specs=in_specs, out_specs=out_specs, check_vma=False
    )
```
